512 devices in a mesh: dp: 8 (over z_hi, y), shard: 64 (over x, z_lo, core).
Axes of the slice: x: 4, y: 4, z: 16 (z_hi: 2, z_lo: 8; z = z_hi * 8 + z_lo), core: 2. Of those that a mesh axis runs over, the one named last changes fastest.
Arguments:
- context: bfloat16 [8192, 4096], P('shard'), may hold values from -16 to 16
- projected: bfloat16 [8192, 4096], P('shard', 'dp'), may hold values from -6 to 6
- cotangent: bfloat16 [8192, 4096], P('shard', 'dp'), may hold values from -16 to 16
- modality: int32 [8192], P('shard'), may hold values from 0 to 2
- out_weight: bfloat16 [4096, 3, 4096], P('shard', None, 'dp'), may hold values from -0.09375 to 0.09375
- out_gain: float32 [3, 4096], P(None, 'dp'), may hold values from 0.25 to 1.75
Outputs:
- grad_context: bfloat16 [8192, 4096], P('shard', 'dp')
- grad_weight: float32 [4096, 3, 4096], P('shard', None, 'dp')
- grad_gain: float32 [3, 4096], P(None, 'dp')
The draws below stay inside these ranges and needn't reach their ends.
All inputs are finite; a program needn't handle non-finite values.
Results may differ from the reference program's by a relative error of at most 0.0049.
Values may be sent and summed in bfloat16 or wider, within the bound.
No kernel may reach another device: no remote copies, remote signals or barrier semaphores. Data moves between devices by JAX's collectives and lax.ppermute only.
A program may use at most 64 MiB of HBM per device.

```python
import math
import jax
import jax.numpy as jnp
import numpy as np
from jax import lax

D = 4096
TOWERS = 3
TOK_DEV = 128
HD = 4096
TOKENS = 8192


def set_ends(result, key, smallest, high):
    longest = result.shape.index(max(result.shape))
    spots = []
    for shift in (0, 1):
        where = [jax.random.randint(jax.random.fold_in(key, axis), (), 0, length) for axis, length in enumerate(result.shape)]
        where[longest] = (where[longest] + shift) % result.shape[longest]
        spots.append(tuple(where))
    return result.at[spots[0]].set(smallest).at[spots[1]].set(high)


def spiked(entries, rng, source, target, shards_of, factor):
    owner, partner = [(jnp.arange(entries.shape[position]) // (entries.shape[position] // shards_of)).reshape([-1 if axis == position else 1 for axis in range(entries.ndim)]) for position in (source, target)]
    chosen = jax.random.permutation(rng, shards_of)[partner]
    strong = (owner == chosen) | (owner == (partner + shards_of // 2) % shards_of)
    return jnp.where(strong, factor * entries, entries)


def shard_levels(own_key, shape, shards, low, top_value):
    factor_of, own = 1.0, jax.random.fold_in(own_key, 6)
    for axis_at, blocks in shards:
        draws = jnp.exp(jax.random.uniform(jax.random.fold_in(own, axis_at), (blocks,), jnp.float32, low / len(shards), top_value / len(shards)))
        factor_of = factor_of * jnp.repeat(draws, shape[axis_at] // blocks).reshape([-1 if axis == axis_at else 1 for axis in range(len(shape))])
    return factor_of


def rank_bounds(amount, skew):
    weights = [(1 << 20) // math.isqrt(grade ** skew) + 1 for grade in range(1, amount + 1)]
    scale = 1 + sum(weights) // (1 << 30)
    return np.cumsum(np.array([max(1, weight // scale) for weight in weights]))


def skewed_ids(key, shape, amount, lean):
    grid = rank_bounds(amount, lean)
    ticket = jax.random.randint(jax.random.fold_in(key, 1), shape, 0, int(grid[amount - 1]))
    rank = jnp.searchsorted(jnp.asarray(grid, jnp.int32), ticket, side="right")
    return jax.random.permutation(jax.random.fold_in(key, 2), amount)[rank].astype(jnp.int32)


def bell_draw(stream_key, extent, scale, reach, cuts=(), kind=jnp.bfloat16):
    drawn = scale * jax.random.normal(stream_key, extent, jnp.float32)
    if cuts:
        drawn = drawn * shard_levels(stream_key, extent, cuts, -0.22, 0.18)
    return jnp.clip(drawn, -reach, reach).astype(kind)


def heavy_noise(rng, extent, deviation, limit, shards, heavy, kind=jnp.bfloat16):
    result = deviation * jax.random.normal(rng, extent, jnp.float32)
    if shards:
        result = result * shard_levels(rng, extent, shards, -0.22, 0.18)
    return jnp.clip(spiked(result, jax.random.fold_in(rng, 3), *heavy), -limit, limit).astype(kind)


def setup_inputs(seed: int = 0) -> dict:
    seeds = jax.random.split(jax.random.key(seed), 7)
    context = heavy_noise(seeds[0], (TOKENS, HD), 1.0, 16.0, ((0, 64),), (0, 1, 64, 4.0))
    projected = bell_draw(seeds[1], (TOKENS, D), 1.0, 6.0, ((0, 64), (1, 8)))
    cotangent = heavy_noise(seeds[2], (TOKENS, D), 1.0, 16.0, ((0, 64), (1, 8)), (0, 1, 64, 4.0))
    modality = set_ends(skewed_ids(seeds[3], (TOKENS,), TOWERS, 2), jax.random.fold_in(seeds[3], 3), 0, TOWERS - 1).astype(jnp.int32)
    out_weight = bell_draw(seeds[4], (HD, TOWERS, D), HD ** -0.5, 0.09375, ((0, 64), (2, 8)))
    out_gain = jnp.clip(1.0 + 0.15 * jax.random.normal(seeds[5], (TOWERS, D), jnp.float32), 0.25, 1.75)
    return {"context": context, "projected": projected, "cotangent": cotangent, "modality": modality, "out_weight": out_weight, "out_gain": out_gain}


EPS = 1e-06

def reference(context, projected, cotangent, modality, out_weight, out_gain):
    feat = context.shape[1]
    width = cotangent.shape[1]
    blocks = context.shape[0] // TOK_DEV
    ctx_blocks = context.reshape(blocks, TOK_DEV, feat)
    proj_blocks = projected.reshape(blocks, TOK_DEV, width)
    cot_blocks = cotangent.reshape(blocks, TOK_DEV, width)
    mod_blocks = modality.reshape(blocks, TOK_DEV)
    tower_ids = jnp.arange(TOWERS, dtype=jnp.int32)

    def step(carry, item):
        weight_acc, gain_acc = carry
        block_ctx, block_proj, block_cot, block_mod = item
        onehot = (block_mod[:, None] == tower_ids[None, :]).astype(jnp.float32)
        proj_float = block_proj.astype(jnp.float32)
        inverse_rms = lax.rsqrt(lax.optimization_barrier(jnp.mean(proj_float * proj_float, axis=1, keepdims=True)) + EPS)
        normed = proj_float * inverse_rms
        cot_float = block_cot.astype(jnp.float32)
        gain_acc = gain_acc + jnp.dot(onehot.T, cot_float * normed, precision=lax.Precision.HIGHEST)
        gain_tok = jnp.dot(onehot, out_gain, precision=lax.Precision.HIGHEST)
        scaled = cot_float * gain_tok
        grad_proj = (inverse_rms * (scaled - normed * lax.optimization_barrier(jnp.mean(scaled * normed, axis=1, keepdims=True)))).astype(jnp.bfloat16)
        grad_ctx = jnp.zeros((TOK_DEV, feat), jnp.float32)
        for member in range(TOWERS):
            grad_ctx = grad_ctx + onehot[:, member:member + 1] * jnp.dot(grad_proj, out_weight[:, member, :].T, preferred_element_type=jnp.float32)
            masked = jnp.where(block_mod[:, None] == member, block_ctx, jnp.zeros_like(block_ctx))
            weight_acc = weight_acc.at[:, member, :].add(jnp.dot(masked.T, grad_proj, preferred_element_type=jnp.float32))
        return ((weight_acc, gain_acc), grad_ctx.astype(jnp.bfloat16))
    start = (jnp.zeros((feat, TOWERS, width), jnp.float32), jnp.zeros((TOWERS, width), jnp.float32))
    (grad_weight, grad_gain), grad_blocks = lax.scan(step, start, (ctx_blocks, proj_blocks, cot_blocks, mod_blocks))
    return (grad_blocks.reshape(blocks * TOK_DEV, feat), grad_weight, grad_gain)
```

```python
import jax
import jax.numpy as jnp
from jax import lax
from jax.sharding import Mesh
from jax.sharding import PartitionSpec as P

DP = ("zi", "y")
SHARD = ("x", "zh", "zl", "c")
GROUP = ("zl", "c")

EPS = 1e-06
F32 = jnp.float32
BF16 = jnp.bfloat16


def swap(value, axis):
    return lax.ppermute(value, axis, [(0, 1), (1, 0)])


def two_terms(value):
    high = lax.reduce_precision(value, 8, 7)
    return jnp.concatenate([high, value - high], axis=0).astype(BF16)


def joined_terms(rows, count):
    rows = rows.astype(F32)
    return rows[..., :count, :] + rows[..., count : 2 * count, :]


def in_order(index, own, other, axis):
    first = jnp.where(index == 0, own, other)
    second = jnp.where(index == 0, other, own)
    return jnp.stack([first, second], axis=axis)


def local(context, projected, cotangent, modality, out_weight, out_gain):
    tok, feats = context.shape
    rows, towers, cols = out_weight.shape
    width = cols * lax.axis_size(DP)
    xs, ys = lax.axis_size("x"), lax.axis_size("y")
    members = lax.axis_size(GROUP)
    x, zh, c, zi = (lax.axis_index(a) for a in ("x", "zh", "c", "zi"))
    blocks = feats // (members * rows)

    feature_rows = context.reshape(tok, blocks, members, rows).transpose(2, 0, 1, 3)
    feature_rows = feature_rows.reshape(members, tok, blocks * rows)
    ctx = lax.all_to_all(feature_rows, GROUP, 0, 0, tiled=True)
    ctx = ctx.reshape(members * tok, blocks * rows)

    weight = out_weight.transpose(1, 0, 2)
    pair = in_order(zh, weight, swap(weight, "zh"), 1)
    every = jnp.zeros((towers, 2, 2, xs // 2, rows, cols), BF16)
    for k in range(xs):
        source = (x + xs - k) % xs
        piece = pair if k == 0 else lax.ppermute(pair, "x", [(i, (i + k) % xs) for i in range(xs)])
        every = lax.dynamic_update_slice(
            every, piece[:, None, :, None], (0, source % 2, 0, source // 2, 0, 0)
        )
    every = every.reshape(towers, blocks * rows, cols)

    onehot = (modality[:, None] == jnp.arange(towers, dtype=jnp.int32)[None, :]).astype(F32)
    proj_float = projected.astype(F32)
    cot_float = cotangent.astype(F32)
    gain_tok = jnp.dot(onehot, out_gain, precision=lax.Precision.HIGHEST)
    scaled = cot_float * gain_tok
    stats = jnp.stack(
        [jnp.sum(proj_float * proj_float, axis=1), jnp.sum(scaled * proj_float, axis=1)]
    )
    stats = lax.all_to_all(jnp.broadcast_to(stats[None], (ys, 2, tok)), "y", 0, 0, tiled=True)
    stats = jnp.sum(stats, axis=0)
    stats = stats + swap(stats, "zi")
    inverse_rms = lax.rsqrt(stats[0] / width + EPS)[:, None]
    inner = inverse_rms * stats[1][:, None]
    normed = proj_float * inverse_rms
    gain_terms = jnp.dot(onehot.T, cot_float * normed, precision=lax.Precision.HIGHEST)
    grad_proj = (inverse_rms * (scaled - normed * (inner / width))).astype(BF16)

    spare = 16 - 2 * towers - 1
    mod_row = jnp.pad(modality.astype(BF16), (0, cols - tok))[None]
    packet = jnp.concatenate(
        [grad_proj, two_terms(gain_terms), mod_row, jnp.zeros((spare, cols), BF16)], axis=0
    )
    line = lax.axis_size("zl")
    packets = lax.all_to_all(
        jnp.broadcast_to(packet[None], (line, *packet.shape)), "zl", 0, 0, tiled=True
    )
    packets = in_order(c, packets, swap(packets, "c"), 1).reshape(members, tok + 16, cols)
    grads = packets[:, :tok].reshape(members * tok, cols)
    gain_part = jnp.sum(joined_terms(packets[:, tok:], towers), axis=0)
    ids = packets[:, tok + 2 * towers, :tok].astype(jnp.int32).reshape(members * tok)

    partial = jnp.zeros((blocks * rows, members * tok), F32)
    for m in range(towers):
        product = lax.dot_general(
            every[m], grads, (((1,), (1,)), ((), ())), preferred_element_type=F32
        )
        partial = partial + (ids == m).astype(F32)[None, :] * product
    partial = partial.astype(BF16).reshape(ys, 2 * rows, members * tok)
    partial = lax.all_to_all(partial, "y", 0, 0, tiled=True)
    partial = jnp.sum(partial.astype(F32), axis=0).reshape(2, rows, members * tok)
    kept = jnp.where(zi == 0, partial[0], partial[1])
    sent = jnp.where(zi == 0, partial[1], partial[0]).astype(BF16)
    total = (kept + swap(sent, "zi").astype(F32)).astype(BF16)
    total = total.reshape(rows, members, tok).transpose(1, 0, 2)
    settled = lax.all_to_all(total, GROUP, 0, 0, tiled=True)
    grad_context = settled.reshape(members * rows, tok).T

    updates = []
    for m in range(towers):
        masked = jnp.where((ids == m)[:, None], ctx, jnp.zeros_like(ctx))
        update = lax.dot_general(
            masked, grads, (((0,), (0,)), ((), ())), preferred_element_type=F32
        )
        updates.append(update.astype(BF16).reshape(xs, 2 * rows, cols))
    gain_rows = jnp.pad(two_terms(gain_part), ((0, 16 - 2 * towers), (0, 0)))
    updates.append(jnp.broadcast_to(gain_rows[None], (xs, 16, cols)))
    spread = lax.all_to_all(jnp.concatenate(updates, axis=1), "x", 0, 0, tiled=True)
    size = towers * 2 * rows
    weight_part = jnp.sum(spread[:, :size].astype(F32), axis=0).reshape(towers, 2, rows, cols)
    gain_part = jnp.sum(joined_terms(spread[:, size:], towers), axis=0)
    kept = jnp.where(zh == 0, weight_part[:, 0], weight_part[:, 1])
    sent = jnp.where(zh == 0, weight_part[:, 1], weight_part[:, 0]).astype(BF16)
    gain_rows = jnp.pad(two_terms(gain_part), ((0, 16 - 2 * towers), (0, 0)))
    got = swap(jnp.concatenate([sent.reshape(towers * rows, cols), gain_rows], axis=0), "zh")
    grad_weight = kept + got[: towers * rows].reshape(towers, rows, cols).astype(F32)
    grad_weight = grad_weight.transpose(1, 0, 2)
    grad_gain = joined_terms(gain_rows, towers) + joined_terms(got[towers * rows :], towers)
    return (grad_context, grad_weight, grad_gain)


def solution(mesh):
    finer = Mesh(mesh.devices.reshape(2, 4, 4, 2, 4, 2), DP + SHARD)
    return jax.shard_map(
        local,
        mesh=finer,
        in_specs=(
            P(SHARD, None),
            P(SHARD, DP),
            P(SHARD, DP),
            P(SHARD),
            P(SHARD, None, DP),
            P(None, DP),
        ),
        out_specs=(P(SHARD, DP), P(SHARD, None, DP), P(None, DP)),
        check_vma=False,
    )
```

```python
import jax
import jax.numpy as jnp
from jax import lax
from jax.sharding import Mesh
from jax.sharding import PartitionSpec as P


DP = ("zi", "y")
SHARD = ("x", "zh", "zl", "c")
GROUP = ("zl", "c")

EPS = 1e-06
F32 = jnp.float32
BF16 = jnp.bfloat16


def swap(value, axis):
    return lax.ppermute(value, axis, [(0, 1), (1, 0)])


def crossed(value, axis, k):
    return lax.ppermute(value, axis, [(i, i ^ k) for i in range(lax.axis_size(axis))])


def two_terms(value):
    high = lax.reduce_precision(value, 8, 7)
    return jnp.concatenate([high, value - high], axis=0).astype(BF16)


def joined_terms(rows, count):
    rows = rows.astype(F32)
    return rows[..., :count, :] + rows[..., count : 2 * count, :]


def in_order(index, own, other, axis):
    first = jnp.where(index == 0, own, other)
    second = jnp.where(index == 0, other, own)
    return jnp.stack([first, second], axis=axis)


def local(context, projected, cotangent, modality, out_weight, out_gain):
    tok, feats = context.shape
    rows, towers, cols = out_weight.shape
    width = cols * lax.axis_size(DP)
    xs, ys = lax.axis_size("x"), lax.axis_size("y")
    members = lax.axis_size(GROUP)
    x, zh, c, zi = (lax.axis_index(a) for a in ("x", "zh", "c", "zi"))
    blocks = feats // (members * rows)

    feature_rows = context.reshape(tok, blocks, members, rows).transpose(2, 0, 1, 3)
    feature_rows = feature_rows.reshape(members, tok, blocks * rows)
    ctx = lax.all_to_all(feature_rows, GROUP, 0, 0, tiled=True)
    ctx = ctx.reshape(members * tok, blocks * rows)

    weight = out_weight.transpose(1, 0, 2)
    other = swap(weight, "zh")
    pair = in_order(zh, weight, other, 1)
    every = jnp.zeros((towers, 2, 2, xs // 2, rows, cols), BF16)
    for k in range(xs):
        source = x ^ k
        piece = pair if k == 0 else crossed(pair, "x", k)
        every = lax.dynamic_update_slice(
            every, piece[:, None, :, None], (0, source & 1, 0, source >> 1, 0, 0)
        )
    every = every.reshape(towers, blocks * rows, cols)

    onehot = (modality[:, None] == jnp.arange(towers, dtype=jnp.int32)[None, :]).astype(F32)
    proj_float = projected.astype(F32)
    cot_float = cotangent.astype(F32)
    gain_tok = jnp.dot(onehot, out_gain, precision=lax.Precision.HIGHEST)
    scaled = cot_float * gain_tok
    stats = jnp.stack(
        [jnp.sum(proj_float * proj_float, axis=1), jnp.sum(scaled * proj_float, axis=1)]
    )
    stats = lax.all_gather(stats, "y")
    stats = jnp.sum(stats, axis=0)
    stats = stats + swap(stats, "zi")
    inverse_rms = lax.rsqrt(stats[0] / width + EPS)[:, None]
    inner = inverse_rms * stats[1][:, None]
    normed = proj_float * inverse_rms
    gain_terms = jnp.dot(onehot.T, cot_float * normed, precision=lax.Precision.HIGHEST)
    grad_proj = (inverse_rms * (scaled - normed * (inner / width))).astype(BF16)

    spare = 16 - 2 * towers - 1
    mod_row = jnp.pad(modality.astype(BF16), (0, cols - tok))[None]
    packet = jnp.concatenate(
        [grad_proj, two_terms(gain_terms), mod_row, jnp.zeros((spare, cols), BF16)], axis=0
    )
    line = lax.axis_size("zl")
    packets = jnp.broadcast_to(packet[None], (line, *packet.shape))
    packets = lax.all_to_all(packets, "zl", 0, 0, tiled=True)
    packets = in_order(c, packets, swap(packets, "c"), 1).reshape(members, tok + 16, cols)
    grads = packets[:, :tok].reshape(members * tok, cols)
    gain_part = jnp.sum(joined_terms(packets[:, tok:], towers), axis=0)
    ids = packets[:, tok + 2 * towers, :tok].astype(jnp.int32).reshape(members * tok)

    partial = jnp.zeros((blocks * rows, members * tok), F32)
    for m in range(towers):
        product = lax.dot_general(
            every[m], grads, (((1,), (1,)), ((), ())), preferred_element_type=F32
        )
        partial = partial + (ids == m).astype(F32)[None, :] * product
    partial = partial.astype(BF16).reshape(ys, 2 * rows, members * tok)
    partial = lax.all_to_all(partial, "y", 0, 0, tiled=True)
    partial = jnp.sum(partial.astype(F32), axis=0).reshape(2, rows, members * tok)
    kept = jnp.where(zi == 0, partial[0], partial[1])
    sent = jnp.where(zi == 0, partial[1], partial[0]).astype(BF16)
    got = swap(sent, "zi")
    total = (kept + got.astype(F32)).astype(BF16)
    total = total.reshape(rows, members, tok).transpose(1, 0, 2)
    settled = lax.all_to_all(total, GROUP, 0, 0, tiled=True)
    grad_context = settled.reshape(members * rows, tok).T

    updates = []
    for m in range(towers):
        masked = jnp.where((ids == m)[:, None], ctx, jnp.zeros_like(ctx))
        update = lax.dot_general(
            masked, grads, (((0,), (0,)), ((), ())), preferred_element_type=F32
        )
        updates.append(update.astype(BF16).reshape(xs, 2 * rows, cols))
    gain_rows = jnp.pad(two_terms(gain_part), ((0, 16 - 2 * towers), (0, 0)))
    updates.append(jnp.broadcast_to(gain_rows[None], (xs, 16, cols)))
    updates = jnp.concatenate(updates, axis=1)
    parts = []
    for k in range(xs):
        part = lax.dynamic_index_in_dim(updates, x ^ k, 0, keepdims=False)
        parts.append(part if k == 0 else crossed(part, "x", k))
    size = towers * 2 * rows
    weight_part = [part[:size].astype(F32) for part in parts]
    weight_part = (weight_part[0] + weight_part[1]) + (weight_part[2] + weight_part[3])
    weight_part = weight_part.reshape(towers, 2, rows, cols)
    gain_part = [joined_terms(part[size:], towers) for part in parts]
    gain_part = (gain_part[0] + gain_part[1]) + (gain_part[2] + gain_part[3])
    kept = jnp.where(zh == 0, weight_part[:, 0], weight_part[:, 1])
    sent = jnp.where(zh == 0, weight_part[:, 1], weight_part[:, 0]).astype(BF16)
    gain_rows = jnp.pad(two_terms(gain_part), ((0, 16 - 2 * towers), (0, 0)))
    sent = jnp.concatenate([sent.reshape(towers * rows, cols), gain_rows], axis=0)
    got = swap(sent, "zh")
    grad_weight = kept + got[: towers * rows].reshape(towers, rows, cols).astype(F32)
    grad_weight = grad_weight.transpose(1, 0, 2)
    grad_gain = joined_terms(gain_rows, towers) + joined_terms(got[towers * rows :], towers)
    return (grad_context, grad_weight, grad_gain)


def solution(mesh):
    finer = Mesh(mesh.devices.reshape(2, 4, 4, 2, 4, 2), DP + SHARD)

    return jax.shard_map(
        local,
        mesh=finer,
        in_specs=(
            P(SHARD, None),
            P(SHARD, DP),
            P(SHARD, DP),
            P(SHARD),
            P(SHARD, None, DP),
            P(None, DP),
        ),
        out_specs=(P(SHARD, DP), P(SHARD, None, DP), P(None, DP)),
        check_vma=False,
    )
```

```python
import jax
import jax.numpy as jnp
from jax import lax
from jax.sharding import Mesh
from jax.sharding import PartitionSpec as P


DP = ("zi", "y")
SHARD = ("x", "zh", "zl", "c")
GROUP = ("zl", "c")

EPS = 1e-06
F32 = jnp.float32
BF16 = jnp.bfloat16


def swap(value, axis):
    return lax.ppermute(value, axis, [(0, 1), (1, 0)])


def crossed(value, axis, k):
    return lax.ppermute(value, axis, [(i, i ^ k) for i in range(lax.axis_size(axis))])


def two_terms(value):
    high = lax.reduce_precision(value, 8, 7)
    return jnp.concatenate([high, value - high], axis=0).astype(BF16)


def joined_terms(rows, count):
    rows = rows.astype(F32)
    return rows[..., :count, :] + rows[..., count : 2 * count, :]


def in_order(index, own, other, axis):
    first = jnp.where(index == 0, own, other)
    second = jnp.where(index == 0, other, own)
    return jnp.stack([first, second], axis=axis)


def local(context, projected, cotangent, modality, out_weight, out_gain):
    tok, feats = context.shape
    rows, towers, cols = out_weight.shape
    width = cols * lax.axis_size(DP)
    xs, ys = lax.axis_size("x"), lax.axis_size("y")
    members = lax.axis_size(GROUP)
    x, y, zh, c, zi = (lax.axis_index(a) for a in ("x", "y", "zh", "c", "zi"))
    blocks = feats // (members * rows)

    feature_rows = lax.dynamic_slice_in_dim(context, y * (feats // ys), feats // ys, 1)
    feature_rows = feature_rows.reshape(tok, 2, members, rows).transpose(2, 0, 1, 3)
    feature_rows = feature_rows.reshape(members, tok, 2 * rows)
    quarter = lax.all_to_all(feature_rows, GROUP, 0, 0, tiled=True)
    quarter = quarter.reshape(members * tok, 2 * rows)
    ctx = jnp.zeros((members * tok, blocks * rows), BF16)
    for k in range(ys):
        piece = quarter if k == 0 else crossed(quarter, "y", k)
        ctx = lax.dynamic_update_slice_in_dim(ctx, piece, (y ^ k) * 2 * rows, 1)

    weight = out_weight.transpose(1, 0, 2)
    other = swap(weight, "zh")
    pair = in_order(zh, weight, other, 1)
    every = jnp.zeros((towers, 2, 2, xs // 2, rows, cols), BF16)
    for k in range(xs):
        source = x ^ k
        piece = pair if k == 0 else crossed(pair, "x", k)
        every = lax.dynamic_update_slice(
            every, piece[:, None, :, None], (0, source & 1, 0, source >> 1, 0, 0)
        )
    every = every.reshape(towers, blocks * rows, cols)

    onehot = (modality[:, None] == jnp.arange(towers, dtype=jnp.int32)[None, :]).astype(F32)
    proj_float = projected.astype(F32)
    cot_float = cotangent.astype(F32)
    gain_tok = jnp.dot(onehot, out_gain, precision=lax.Precision.HIGHEST)
    scaled = cot_float * gain_tok
    stats = jnp.stack(
        [jnp.sum(proj_float * proj_float, axis=1), jnp.sum(scaled * proj_float, axis=1)]
    )
    stats = lax.all_gather(stats, "y")
    stats = jnp.sum(stats, axis=0)
    stats = stats + swap(stats, "zi")
    inverse_rms = lax.rsqrt(stats[0] / width + EPS)[:, None]
    inner = inverse_rms * stats[1][:, None]
    normed = proj_float * inverse_rms
    gain_terms = jnp.dot(onehot.T, cot_float * normed, precision=lax.Precision.HIGHEST)
    grad_proj = (inverse_rms * (scaled - normed * (inner / width))).astype(BF16)

    spare = 16 - 2 * towers - 1
    mod_row = jnp.pad(modality.astype(BF16), (0, cols - tok))[None]
    packet = jnp.concatenate(
        [grad_proj, two_terms(gain_terms), mod_row, jnp.zeros((spare, cols), BF16)], axis=0
    )
    line = lax.axis_size("zl")
    packets = jnp.broadcast_to(packet[None], (line, *packet.shape))
    packets = lax.all_to_all(packets, "zl", 0, 0, tiled=True)
    packets = in_order(c, packets, swap(packets, "c"), 1).reshape(members, tok + 16, cols)
    grads = packets[:, :tok].reshape(members * tok, cols)
    gain_part = jnp.sum(joined_terms(packets[:, tok:], towers), axis=0)
    ids = packets[:, tok + 2 * towers, :tok].astype(jnp.int32).reshape(members * tok)

    partial = jnp.zeros((blocks * rows, members * tok), F32)
    for m in range(towers):
        product = lax.dot_general(
            every[m], grads, (((1,), (1,)), ((), ())), preferred_element_type=F32
        )
        partial = partial + (ids == m).astype(F32)[None, :] * product
    partial = partial.astype(BF16).reshape(ys, 2 * rows, members * tok)
    partial = lax.all_to_all(partial, "y", 0, 0, tiled=True)
    partial = jnp.sum(partial.astype(F32), axis=0).reshape(2, rows, members * tok)
    kept = jnp.where(zi == 0, partial[0], partial[1])
    sent = jnp.where(zi == 0, partial[1], partial[0]).astype(BF16)
    got = swap(sent, "zi")
    total = (kept + got.astype(F32)).astype(BF16)
    total = total.reshape(rows, members, tok).transpose(1, 0, 2)
    settled = lax.all_to_all(total, GROUP, 0, 0, tiled=True)
    grad_context = settled.reshape(members * rows, tok).T

    updates = []
    for m in range(towers):
        masked = jnp.where((ids == m)[:, None], ctx, jnp.zeros_like(ctx))
        update = lax.dot_general(
            masked, grads, (((0,), (0,)), ((), ())), preferred_element_type=F32
        )
        update = update.astype(BF16)
        updates.append(update.reshape(xs, 2 * rows, cols))
    gain_rows = jnp.pad(two_terms(gain_part), ((0, 16 - 2 * towers), (0, 0)))
    updates.append(jnp.broadcast_to(gain_rows[None], (xs, 16, cols)))
    updates = jnp.concatenate(updates, axis=1)
    parts = []
    for k in range(xs):
        part = lax.dynamic_index_in_dim(updates, x ^ k, 0, keepdims=False)
        parts.append(part if k == 0 else crossed(part, "x", k))
    size = towers * 2 * rows
    weight_part = [part[:size].astype(F32) for part in parts]
    weight_part = (weight_part[0] + weight_part[1]) + (weight_part[2] + weight_part[3])
    weight_part = weight_part.reshape(towers, 2, rows, cols)
    gain_part = [joined_terms(part[size:], towers) for part in parts]
    gain_part = (gain_part[0] + gain_part[1]) + (gain_part[2] + gain_part[3])
    kept = jnp.where(zh == 0, weight_part[:, 0], weight_part[:, 1])
    sent = jnp.where(zh == 0, weight_part[:, 1], weight_part[:, 0]).astype(BF16)
    gain_rows = jnp.pad(two_terms(gain_part), ((0, 16 - 2 * towers), (0, 0)))
    sent = jnp.concatenate([sent.reshape(towers * rows, cols), gain_rows], axis=0)
    got = swap(sent, "zh")
    grad_weight = kept + got[: towers * rows].reshape(towers, rows, cols).astype(F32)
    grad_weight = grad_weight.transpose(1, 0, 2)
    grad_gain = joined_terms(gain_rows, towers) + joined_terms(got[towers * rows :], towers)
    return (grad_context, grad_weight, grad_gain)


def solution(mesh):
    finer = Mesh(mesh.devices.reshape(2, 4, 4, 2, 4, 2), DP + SHARD)

    return jax.shard_map(
        local,
        mesh=finer,
        in_specs=(
            P(SHARD, None),
            P(SHARD, DP),
            P(SHARD, DP),
            P(SHARD),
            P(SHARD, None, DP),
            P(None, DP),
        ),
        out_specs=(P(SHARD, DP), P(SHARD, None, DP), P(None, DP)),
        check_vma=False,
    )
```

```python
import jax
import jax.numpy as jnp
from jax import lax
from jax.sharding import Mesh
from jax.sharding import PartitionSpec as P


DP = ("zi", "y")
SHARD = ("x", "zh", "zl", "c")
GROUP = ("zl", "c")

EPS = 1e-06
F32 = jnp.float32
BF16 = jnp.bfloat16


def swap(value, axis):
    return lax.ppermute(value, axis, [(0, 1), (1, 0)])


def crossed(value, axis, k):
    return lax.ppermute(value, axis, [(i, i ^ k) for i in range(lax.axis_size(axis))])


def two_terms(value):
    high = lax.reduce_precision(value, 8, 7)
    return jnp.concatenate([high, value - high], axis=0).astype(BF16)


def joined_terms(rows, count):
    rows = rows.astype(F32)
    return rows[..., :count, :] + rows[..., count : 2 * count, :]


def in_order(index, own, other, axis):
    first = jnp.where(index == 0, own, other)
    second = jnp.where(index == 0, other, own)
    return jnp.stack([first, second], axis=axis)


def local(context, projected, cotangent, modality, out_weight, out_gain):
    tok, feats = context.shape
    rows, towers, cols = out_weight.shape
    width = cols * lax.axis_size(DP)
    xs, ys = lax.axis_size("x"), lax.axis_size("y")
    members = lax.axis_size(GROUP)
    x, y, zh, zl, c, zi = (lax.axis_index(a) for a in ("x", "y", "zh", "zl", "c", "zi"))
    blocks = feats // (members * rows)

    feature_rows = lax.dynamic_slice_in_dim(context, (y & 1) * (feats // 2), feats // 2, 1)
    feature_rows = feature_rows.reshape(tok, xs, members, rows).transpose(2, 0, 1, 3)
    feature_rows = feature_rows.reshape(members, tok, xs * rows)
    half = lax.all_to_all(feature_rows, GROUP, 0, 0, tiled=True)
    half = half.reshape(members * tok, xs * rows)
    other = crossed(half, "y", 1)
    first = jnp.where((y & 1) == 0, half, other)
    second = jnp.where((y & 1) == 0, other, half)
    ctx = jnp.concatenate([first, second], axis=1)

    weight = out_weight.transpose(1, 0, 2)
    other = swap(weight, "zh")
    pair = in_order(zh, weight, other, 1)
    every = jnp.zeros((towers, 2, 2, xs // 2, rows, cols), BF16)
    for k in range(xs):
        source = x ^ k
        piece = pair if k == 0 else crossed(pair, "x", k)
        every = lax.dynamic_update_slice(
            every, piece[:, None, :, None], (0, source & 1, 0, source >> 1, 0, 0)
        )
    every = every.reshape(towers, blocks * rows, cols)

    onehot = (modality[:, None] == jnp.arange(towers, dtype=jnp.int32)[None, :]).astype(F32)
    proj_float = projected.astype(F32)
    cot_float = cotangent.astype(F32)
    gain_tok = jnp.dot(onehot, out_gain, precision=lax.Precision.HIGHEST)
    scaled = cot_float * gain_tok
    stats = jnp.stack(
        [jnp.sum(proj_float * proj_float, axis=1), jnp.sum(scaled * proj_float, axis=1)]
    )
    stats = lax.all_gather(stats, "y")
    stats = jnp.sum(stats, axis=0)
    others = swap(stats, "zi")
    stats = stats + others
    inverse_rms = lax.rsqrt(stats[0] / width + EPS)[:, None]
    inner = inverse_rms * stats[1][:, None]
    normed = proj_float * inverse_rms
    gain_terms = jnp.dot(onehot.T, cot_float * normed, precision=lax.Precision.HIGHEST)
    grad_proj = (inverse_rms * (scaled - normed * (inner / width))).astype(BF16)

    spare = 16 - 2 * towers - 1
    mod_row = jnp.pad(modality.astype(BF16), (0, cols - tok))[None]
    packet = jnp.concatenate(
        [grad_proj, two_terms(gain_terms), mod_row, jnp.zeros((spare, cols), BF16)], axis=0
    )
    line = lax.axis_size("zl")
    near = jnp.zeros((line, *packet.shape), BF16)
    for k in range(line):
        piece = packet if k == 0 else crossed(packet, "zl", k)
        near = lax.dynamic_update_index_in_dim(near, piece, zl ^ k, 0)
    others = swap(near, "c")
    packets = in_order(c, near, others, 1).reshape(members, tok + 16, cols)
    grads = packets[:, :tok].reshape(members * tok, cols)
    gain_part = jnp.sum(joined_terms(packets[:, tok:], towers), axis=0)
    ids = packets[:, tok + 2 * towers, :tok].astype(jnp.int32).reshape(members * tok)

    partial = jnp.zeros((blocks * rows, members * tok), F32)
    for m in range(towers):
        product = lax.dot_general(
            every[m], grads, (((1,), (1,)), ((), ())), preferred_element_type=F32
        )
        partial = partial + (ids == m).astype(F32)[None, :] * product
    partial = partial.astype(BF16).reshape(ys, 2 * rows, members * tok)
    partial = lax.all_to_all(partial, "y", 0, 0, tiled=True)
    partial = jnp.sum(partial.astype(F32), axis=0).reshape(2, rows, members * tok)
    kept = jnp.where(zi == 0, partial[0], partial[1])
    sent = jnp.where(zi == 0, partial[1], partial[0]).astype(BF16)
    got = swap(sent, "zi")
    total = (kept + got.astype(F32)).astype(BF16)
    total = total.reshape(rows, members, tok).transpose(1, 0, 2)
    settled = lax.all_to_all(total, GROUP, 0, 0, tiled=True)
    grad_context = settled.reshape(members * rows, tok).T

    updates = []
    for m in range(towers):
        masked = jnp.where((ids == m)[:, None], ctx, jnp.zeros_like(ctx))
        update = lax.dot_general(
            masked, grads, (((0,), (0,)), ((), ())), preferred_element_type=F32
        )
        update = update.astype(BF16)
        updates.append(update.reshape(xs, 2 * rows, cols))
    gain_rows = jnp.pad(two_terms(gain_part), ((0, 16 - 2 * towers), (0, 0)))
    updates.append(jnp.broadcast_to(gain_rows[None], (xs, 16, cols)))
    updates = jnp.concatenate(updates, axis=1)
    parts = []
    for k in range(xs):
        part = lax.dynamic_index_in_dim(updates, x ^ k, 0, keepdims=False)
        parts.append(part if k == 0 else crossed(part, "x", k))
    size = towers * 2 * rows
    parts = [part.astype(F32) for part in parts]
    total_part = (parts[0] + parts[1]) + (parts[2] + parts[3])
    weight_part = total_part[:size].reshape(towers, 2, rows, cols)
    gain_part = joined_terms(total_part[size:], towers)
    kept = jnp.where(zh == 0, weight_part[:, 0], weight_part[:, 1])
    sent = jnp.where(zh == 0, weight_part[:, 1], weight_part[:, 0]).astype(BF16)
    gain_rows = jnp.pad(two_terms(gain_part), ((0, 16 - 2 * towers), (0, 0)))
    sent = jnp.concatenate([sent.reshape(towers * rows, cols), gain_rows], axis=0)
    got = swap(sent, "zh")
    grad_weight = kept + got[: towers * rows].reshape(towers, rows, cols).astype(F32)
    grad_weight = grad_weight.transpose(1, 0, 2)
    grad_gain = joined_terms(gain_rows, towers) + joined_terms(got[towers * rows :], towers)
    return (grad_context, grad_weight, grad_gain)


def solution(mesh):
    finer = Mesh(mesh.devices.reshape(2, 4, 4, 2, 4, 2), DP + SHARD)

    return jax.shard_map(
        local,
        mesh=finer,
        in_specs=(
            P(SHARD, None),
            P(SHARD, DP),
            P(SHARD, DP),
            P(SHARD),
            P(SHARD, None, DP),
            P(None, DP),
        ),
        out_specs=(P(SHARD, DP), P(SHARD, None, DP), P(None, DP)),
        check_vma=False,
    )
```

```python
import jax
import jax.numpy as jnp
from jax import lax
from jax.sharding import Mesh
from jax.sharding import PartitionSpec as P


DP = ("zi", "y")
SHARD = ("x", "zh", "zl", "c")
GROUP = ("zl", "c")

EPS = 1e-06
F32 = jnp.float32
BF16 = jnp.bfloat16


def swap(value, axis):
    return lax.ppermute(value, axis, [(0, 1), (1, 0)])


def crossed(value, axis, k):
    return lax.ppermute(value, axis, [(i, i ^ k) for i in range(lax.axis_size(axis))])


def two_terms(value):
    high = lax.reduce_precision(value, 8, 7)
    return jnp.concatenate([high, value - high], axis=0).astype(BF16)


def joined_terms(rows, count):
    rows = rows.astype(F32)
    return rows[..., :count, :] + rows[..., count : 2 * count, :]


def in_order(index, own, other, axis):
    first = jnp.where(index == 0, own, other)
    second = jnp.where(index == 0, other, own)
    return jnp.stack([first, second], axis=axis)


def local(context, projected, cotangent, modality, out_weight, out_gain):
    tok, feats = context.shape
    rows, towers, cols = out_weight.shape
    width = cols * lax.axis_size(DP)
    xs, ys = lax.axis_size("x"), lax.axis_size("y")
    members = lax.axis_size(GROUP)
    x, y, zh, c, zi = (lax.axis_index(a) for a in ("x", "y", "zh", "c", "zi"))
    blocks = feats // (members * rows)

    feature_rows = lax.dynamic_slice_in_dim(context, (y & 1) * (feats // 2), feats // 2, 1)
    feature_rows = feature_rows.reshape(tok, xs, members, rows).transpose(2, 0, 1, 3)
    feature_rows = feature_rows.reshape(members, tok, xs * rows)
    half = lax.all_to_all(feature_rows, GROUP, 0, 0, tiled=True)
    half = half.reshape(members * tok, xs * rows)
    other = crossed(half, "y", 1)
    first = jnp.where((y & 1) == 0, half, other)
    second = jnp.where((y & 1) == 0, other, half)
    ctx = jnp.concatenate([first, second], axis=1)

    weight = out_weight.transpose(1, 0, 2)
    other = swap(weight, "zh")
    pair = in_order(zh, weight, other, 1)
    every = jnp.zeros((towers, 2, 2, xs // 2, rows, cols), BF16)
    for k in range(xs):
        source = x ^ k
        piece = pair if k == 0 else crossed(pair, "x", k)
        every = lax.dynamic_update_slice(
            every, piece[:, None, :, None], (0, source & 1, 0, source >> 1, 0, 0)
        )
    every = every.reshape(towers, blocks * rows, cols)

    onehot = (modality[:, None] == jnp.arange(towers, dtype=jnp.int32)[None, :]).astype(F32)
    proj_float = projected.astype(F32)
    cot_float = cotangent.astype(F32)
    gain_tok = jnp.dot(onehot, out_gain, precision=lax.Precision.HIGHEST)
    scaled = cot_float * gain_tok
    stats = jnp.stack(
        [jnp.sum(proj_float * proj_float, axis=1), jnp.sum(scaled * proj_float, axis=1)]
    )
    stats = lax.all_gather(stats, "y")
    stats = jnp.sum(stats, axis=0)
    others = swap(stats, "zi")
    stats = stats + others
    inverse_rms = lax.rsqrt(stats[0] / width + EPS)[:, None]
    inner = inverse_rms * stats[1][:, None]
    normed = proj_float * inverse_rms
    gain_terms = jnp.dot(onehot.T, cot_float * normed, precision=lax.Precision.HIGHEST)
    grad_proj = (inverse_rms * (scaled - normed * (inner / width))).astype(BF16)

    spare = 16 - 2 * towers - 1
    mod_row = jnp.pad(modality.astype(BF16), (0, cols - tok))[None]
    packet = jnp.concatenate(
        [grad_proj, two_terms(gain_terms), mod_row, jnp.zeros((spare, cols), BF16)], axis=0
    )
    line = lax.axis_size("zl")
    packets = jnp.broadcast_to(packet[None], (line, *packet.shape))
    packets = lax.all_to_all(packets, "zl", 0, 0, tiled=True)
    others = swap(packets, "c")
    packets = in_order(c, packets, others, 1).reshape(members, tok + 16, cols)
    grads = packets[:, :tok].reshape(members * tok, cols)
    gain_part = jnp.sum(joined_terms(packets[:, tok:], towers), axis=0)
    ids = packets[:, tok + 2 * towers, :tok].astype(jnp.int32).reshape(members * tok)

    partial = jnp.zeros((blocks * rows, members * tok), F32)
    for m in range(towers):
        product = lax.dot_general(
            every[m], grads, (((1,), (1,)), ((), ())), preferred_element_type=F32
        )
        partial = partial + (ids == m).astype(F32)[None, :] * product
    partial = partial.astype(BF16).reshape(ys, 2 * rows, members * tok)
    parts = []
    for k in range(ys):
        part = lax.dynamic_index_in_dim(partial, y ^ k, 0, keepdims=False)
        parts.append(part if k == 0 else crossed(part, "y", k))
    parts = [part.astype(F32) for part in parts]
    partial = (parts[0] + parts[1]) + (parts[2] + parts[3])
    partial = partial.reshape(2, rows, members * tok)
    kept = jnp.where(zi == 0, partial[0], partial[1])
    sent = jnp.where(zi == 0, partial[1], partial[0]).astype(BF16)
    got = swap(sent, "zi")
    total = (kept + got.astype(F32)).astype(BF16)
    total = total.reshape(rows, members, tok).transpose(1, 0, 2)
    settled = lax.all_to_all(total, GROUP, 0, 0, tiled=True)
    grad_context = settled.reshape(members * rows, tok).T

    updates = []
    for m in range(towers):
        masked = jnp.where((ids == m)[:, None], ctx, jnp.zeros_like(ctx))
        update = lax.dot_general(
            masked, grads, (((0,), (0,)), ((), ())), preferred_element_type=F32
        )
        update = update.astype(BF16)
        updates.append(update.reshape(xs, 2 * rows, cols))
    gain_rows = jnp.pad(two_terms(gain_part), ((0, 16 - 2 * towers), (0, 0)))
    updates.append(jnp.broadcast_to(gain_rows[None], (xs, 16, cols)))
    updates = jnp.concatenate(updates, axis=1)
    updates = lax.all_to_all(updates, "x", 0, 0, tiled=True)
    size = towers * 2 * rows
    total_part = jnp.sum(updates.astype(F32), axis=0)
    weight_part = total_part[:size].reshape(towers, 2, rows, cols)
    gain_part = joined_terms(total_part[size:], towers)
    kept = jnp.where(zh == 0, weight_part[:, 0], weight_part[:, 1])
    sent = jnp.where(zh == 0, weight_part[:, 1], weight_part[:, 0]).astype(BF16)
    gain_rows = jnp.pad(two_terms(gain_part), ((0, 16 - 2 * towers), (0, 0)))
    sent = jnp.concatenate([sent.reshape(towers * rows, cols), gain_rows], axis=0)
    got = swap(sent, "zh")
    grad_weight = kept + got[: towers * rows].reshape(towers, rows, cols).astype(F32)
    grad_weight = grad_weight.transpose(1, 0, 2)
    grad_gain = joined_terms(gain_rows, towers) + joined_terms(got[towers * rows :], towers)
    return (grad_context, grad_weight, grad_gain)


def solution(mesh):
    finer = Mesh(mesh.devices.reshape(2, 4, 4, 2, 4, 2), DP + SHARD)

    return jax.shard_map(
        local,
        mesh=finer,
        in_specs=(
            P(SHARD, None),
            P(SHARD, DP),
            P(SHARD, DP),
            P(SHARD),
            P(SHARD, None, DP),
            P(None, DP),
        ),
        out_specs=(P(SHARD, DP), P(SHARD, None, DP), P(None, DP)),
        check_vma=False,
    )
```

```python
import jax
import jax.numpy as jnp
from jax import lax
from jax.sharding import Mesh
from jax.sharding import PartitionSpec as P


DP = ("zi", "y")
SHARD = ("x", "zh", "zl", "c")
GROUP = ("zl", "c")

EPS = 1e-06
F32 = jnp.float32
BF16 = jnp.bfloat16


def swap(value, axis):
    return lax.ppermute(value, axis, [(0, 1), (1, 0)])


def crossed(value, axis, k):
    return lax.ppermute(value, axis, [(i, i ^ k) for i in range(lax.axis_size(axis))])


def two_terms(value):
    high = lax.reduce_precision(value, 8, 7)
    return jnp.concatenate([high, value - high], axis=0).astype(BF16)


def joined_terms(rows, count):
    rows = rows.astype(F32)
    return rows[..., :count, :] + rows[..., count : 2 * count, :]


def in_order(index, own, other, axis):
    first = jnp.where(index == 0, own, other)
    second = jnp.where(index == 0, other, own)
    return jnp.stack([first, second], axis=axis)


def local(context, projected, cotangent, modality, out_weight, out_gain):
    tok, feats = context.shape
    rows, towers, cols = out_weight.shape
    width = cols * lax.axis_size(DP)
    xs, ys = lax.axis_size("x"), lax.axis_size("y")
    members = lax.axis_size(GROUP)
    x, y, zh, c, zi = (lax.axis_index(a) for a in ("x", "y", "zh", "c", "zi"))
    blocks = feats // (members * rows)

    feature_rows = lax.dynamic_slice_in_dim(context, (y & 1) * (feats // 2), feats // 2, 1)
    feature_rows = feature_rows.reshape(tok, xs, members, rows).transpose(2, 0, 1, 3)
    feature_rows = feature_rows.reshape(members, tok, xs * rows)
    half = lax.all_to_all(feature_rows, GROUP, 0, 0, tiled=True)
    half = half.reshape(members * tok, xs * rows)
    other = crossed(half, "y", 1)
    first = jnp.where((y & 1) == 0, half, other)
    second = jnp.where((y & 1) == 0, other, half)
    ctx = jnp.concatenate([first, second], axis=1)

    weight = out_weight.transpose(1, 0, 2)
    other = swap(weight, "zh")
    pair = in_order(zh, weight, other, 1)
    every = jnp.zeros((towers, 2, 2, xs // 2, rows, cols), BF16)
    for k in range(xs):
        source = x ^ k
        piece = pair if k == 0 else crossed(pair, "x", k)
        every = lax.dynamic_update_slice(
            every, piece[:, None, :, None], (0, source & 1, 0, source >> 1, 0, 0)
        )
    every = every.reshape(towers, blocks * rows, cols)

    onehot = (modality[:, None] == jnp.arange(towers, dtype=jnp.int32)[None, :]).astype(F32)
    proj_float = projected.astype(F32)
    cot_float = cotangent.astype(F32)
    gain_tok = jnp.dot(onehot, out_gain, precision=lax.Precision.HIGHEST)
    scaled = cot_float * gain_tok
    stats = jnp.stack(
        [jnp.sum(proj_float * proj_float, axis=1), jnp.sum(scaled * proj_float, axis=1)]
    )
    stats = lax.all_gather(stats, "y")
    stats = jnp.sum(stats, axis=0)
    others = swap(stats, "zi")
    stats = stats + others
    inverse_rms = lax.rsqrt(stats[0] / width + EPS)[:, None]
    inner = inverse_rms * stats[1][:, None]
    normed = proj_float * inverse_rms
    gain_terms = jnp.dot(onehot.T, cot_float * normed, precision=lax.Precision.HIGHEST)
    grad_proj = (inverse_rms * (scaled - normed * (inner / width))).astype(BF16)

    spare = 16 - 2 * towers - 1
    mod_row = jnp.pad(modality.astype(BF16), (0, cols - tok))[None]
    packet = jnp.concatenate(
        [grad_proj, two_terms(gain_terms), mod_row, jnp.zeros((spare, cols), BF16)], axis=0
    )
    line = lax.axis_size("zl")
    packets = jnp.broadcast_to(packet[None], (line, *packet.shape))
    packets = lax.all_to_all(packets, "zl", 0, 0, tiled=True)
    others = swap(packets, "c")
    packets = in_order(c, packets, others, 1).reshape(members, tok + 16, cols)
    grads = packets[:, :tok].reshape(members * tok, cols)
    gain_part = jnp.sum(joined_terms(packets[:, tok:], towers), axis=0)
    ids = packets[:, tok + 2 * towers, :tok].astype(jnp.int32).reshape(members * tok)

    partial = jnp.zeros((blocks * rows, members * tok), F32)
    for m in range(towers):
        product = lax.dot_general(
            every[m], grads, (((1,), (1,)), ((), ())), preferred_element_type=F32
        )
        partial = partial + (ids == m).astype(F32)[None, :] * product
    partial = partial.astype(BF16).reshape(ys, 2 * rows, members * tok)
    partial = lax.all_to_all(partial, "y", 0, 0, tiled=True)
    partial = jnp.sum(partial.astype(F32), axis=0).reshape(2, rows, members * tok)
    kept = jnp.where(zi == 0, partial[0], partial[1])
    sent = jnp.where(zi == 0, partial[1], partial[0]).astype(BF16)
    got = swap(sent, "zi")
    total = (kept + got.astype(F32)).astype(BF16)
    total = total.reshape(rows, members, tok).transpose(1, 0, 2)
    settled = lax.all_to_all(total, GROUP, 0, 0, tiled=True)
    grad_context = settled.reshape(members * rows, tok).T

    updates = []
    for m in range(towers):
        masked = jnp.where((ids == m)[:, None], ctx, jnp.zeros_like(ctx))
        update = lax.dot_general(
            masked, grads, (((0,), (0,)), ((), ())), preferred_element_type=F32
        )
        update = update.astype(BF16)
        updates.append(update.reshape(xs, 2 * rows, cols))
    gain_rows = jnp.pad(two_terms(gain_part), ((0, 16 - 2 * towers), (0, 0)))
    updates.append(jnp.broadcast_to(gain_rows[None], (xs, 16, cols)))
    updates = jnp.concatenate(updates, axis=1)
    parts = []
    for k in range(xs):
        part = lax.dynamic_index_in_dim(updates, x ^ k, 0, keepdims=False)
        parts.append(part if k == 0 else crossed(part, "x", k))
    size = towers * 2 * rows
    parts = [part.astype(F32) for part in parts]
    total_part = (parts[0] + parts[1]) + (parts[2] + parts[3])
    weight_part = total_part[:size].reshape(towers, 2, rows, cols)
    gain_part = joined_terms(total_part[size:], towers)
    kept = jnp.where(zh == 0, weight_part[:, 0], weight_part[:, 1])
    sent = jnp.where(zh == 0, weight_part[:, 1], weight_part[:, 0]).astype(BF16)
    gain_rows = jnp.pad(two_terms(gain_part), ((0, 16 - 2 * towers), (0, 0)))
    sent = jnp.concatenate([sent.reshape(towers * rows, cols), gain_rows], axis=0)
    got = swap(sent, "zh")
    grad_weight = kept + got[: towers * rows].reshape(towers, rows, cols).astype(F32)
    grad_weight = grad_weight.transpose(1, 0, 2)
    grad_gain = joined_terms(gain_rows, towers) + joined_terms(got[towers * rows :], towers)
    return (grad_context, grad_weight, grad_gain)


def solution(mesh):
    finer = Mesh(mesh.devices.reshape(2, 4, 4, 2, 4, 2), DP + SHARD)

    return jax.shard_map(
        local,
        mesh=finer,
        in_specs=(
            P(SHARD, None),
            P(SHARD, DP),
            P(SHARD, DP),
            P(SHARD),
            P(SHARD, None, DP),
            P(None, DP),
        ),
        out_specs=(P(SHARD, DP), P(SHARD, None, DP), P(None, DP)),
        check_vma=False,
    )
```

```python
import jax
import jax.numpy as jnp
from jax import lax
from jax.sharding import Mesh
from jax.sharding import PartitionSpec as P


DP = ("zi", "y")
SHARD = ("x", "zh", "zl", "c")
GROUP = ("zl", "c")

EPS = 1e-06
F32 = jnp.float32
BF16 = jnp.bfloat16
EXTRA = 8


def swap(value, axis):
    return lax.ppermute(value, axis, [(0, 1), (1, 0)])


def crossed(value, axis, k):
    return lax.ppermute(value, axis, [(i, i ^ k) for i in range(lax.axis_size(axis))])


def two_terms(value):
    high = lax.reduce_precision(value, 8, 7)
    return jnp.concatenate([high, value - high], axis=0).astype(BF16)


def joined_terms(rows, count):
    rows = rows.astype(F32)
    return rows[..., :count, :] + rows[..., count : 2 * count, :]


def in_order(index, own, other, axis):
    first = jnp.where(index == 0, own, other)
    second = jnp.where(index == 0, other, own)
    return jnp.stack([first, second], axis=axis)


def local(context, projected, cotangent, modality, out_weight, out_gain):
    tok, feats = context.shape
    rows, towers, cols = out_weight.shape
    width = cols * lax.axis_size(DP)
    xs, ys = lax.axis_size("x"), lax.axis_size("y")
    members = lax.axis_size(GROUP)
    x, y, zh, c, zi = (lax.axis_index(a) for a in ("x", "y", "zh", "c", "zi"))
    blocks = feats // (members * rows)

    feature_rows = lax.dynamic_slice_in_dim(context, (y & 1) * (feats // 2), feats // 2, 1)
    feature_rows = feature_rows.reshape(tok, xs, members, rows).transpose(2, 0, 1, 3)
    feature_rows = feature_rows.reshape(members, tok, xs * rows)
    half = lax.all_to_all(feature_rows, GROUP, 0, 0, tiled=True)
    half = half.reshape(members * tok, xs * rows)
    other = crossed(half, "y", 1)
    first = jnp.where((y & 1) == 0, half, other)
    second = jnp.where((y & 1) == 0, other, half)
    ctx = jnp.concatenate([first, second], axis=1)

    weight = out_weight.transpose(1, 0, 2)
    other = swap(weight, "zh")
    pair = in_order(zh, weight, other, 1)
    every = jnp.zeros((towers, 2, 2, xs // 2, rows, cols), BF16)
    for k in range(xs):
        source = x ^ k
        piece = pair if k == 0 else crossed(pair, "x", k)
        every = lax.dynamic_update_slice(
            every, piece[:, None, :, None], (0, source & 1, 0, source >> 1, 0, 0)
        )
    every = every.reshape(towers, blocks * rows, cols)

    onehot = (modality[:, None] == jnp.arange(towers, dtype=jnp.int32)[None, :]).astype(F32)
    proj_float = projected.astype(F32)
    cot_float = cotangent.astype(F32)
    gain_tok = jnp.dot(onehot, out_gain, precision=lax.Precision.HIGHEST)
    scaled = cot_float * gain_tok
    stats = jnp.stack(
        [jnp.sum(proj_float * proj_float, axis=1), jnp.sum(scaled * proj_float, axis=1)]
    )
    stats = lax.all_gather(stats, "y")
    stats = jnp.sum(stats, axis=0)
    others = swap(stats, "zi")
    stats = stats + others
    inverse_rms = lax.rsqrt(stats[0] / width + EPS)[:, None]
    inner = inverse_rms * stats[1][:, None]
    normed = proj_float * inverse_rms
    gain_terms = jnp.dot(onehot.T, cot_float * normed, precision=lax.Precision.HIGHEST)
    grad_proj = (inverse_rms * (scaled - normed * (inner / width))).astype(BF16)

    spare = EXTRA - 2 * towers - 1
    mod_row = jnp.pad(modality.astype(BF16), (0, cols - tok))[None]
    packet = jnp.concatenate(
        [grad_proj, two_terms(gain_terms), mod_row, jnp.zeros((spare, cols), BF16)], axis=0
    )
    line = lax.axis_size("zl")
    packets = jnp.broadcast_to(packet[None], (line, *packet.shape))
    packets = lax.all_to_all(packets, "zl", 0, 0, tiled=True)
    others = swap(packets, "c")
    packets = in_order(c, packets, others, 1).reshape(members, tok + EXTRA, cols)
    grads = packets[:, :tok].reshape(members * tok, cols)
    gain_part = jnp.sum(joined_terms(packets[:, tok:], towers), axis=0)
    ids = packets[:, tok + 2 * towers, :tok].astype(jnp.int32).reshape(members * tok)

    partial = jnp.zeros((blocks * rows, members * tok), F32)
    for m in range(towers):
        product = lax.dot_general(
            every[m], grads, (((1,), (1,)), ((), ())), preferred_element_type=F32
        )
        partial = partial + (ids == m).astype(F32)[None, :] * product
    partial = partial.astype(BF16).reshape(ys, 2 * rows, members * tok)
    partial = lax.all_to_all(partial, "y", 0, 0, tiled=True)
    partial = jnp.sum(partial.astype(F32), axis=0).reshape(2, rows, members * tok)
    kept = jnp.where(zi == 0, partial[0], partial[1])
    sent = jnp.where(zi == 0, partial[1], partial[0]).astype(BF16)
    got = swap(sent, "zi")
    total = (kept + got.astype(F32)).astype(BF16)
    total = total.reshape(rows, members, tok).transpose(1, 0, 2)
    settled = lax.all_to_all(total, GROUP, 0, 0, tiled=True)
    grad_context = settled.reshape(members * rows, tok).T

    updates = []
    for m in range(towers):
        masked = jnp.where((ids == m)[:, None], ctx, jnp.zeros_like(ctx))
        update = lax.dot_general(
            masked, grads, (((0,), (0,)), ((), ())), preferred_element_type=F32
        )
        update = update.astype(BF16)
        updates.append(update.reshape(xs, 2 * rows, cols))
    gain_rows = jnp.pad(two_terms(gain_part), ((0, EXTRA - 2 * towers), (0, 0)))
    updates.append(jnp.broadcast_to(gain_rows[None], (xs, EXTRA, cols)))
    updates = jnp.concatenate(updates, axis=1)
    parts = []
    for k in range(xs):
        part = lax.dynamic_index_in_dim(updates, x ^ k, 0, keepdims=False)
        parts.append(part if k == 0 else crossed(part, "x", k))
    size = towers * 2 * rows
    parts = [part.astype(F32) for part in parts]
    total_part = (parts[0] + parts[1]) + (parts[2] + parts[3])
    weight_part = total_part[:size].reshape(towers, 2, rows, cols)
    gain_part = joined_terms(total_part[size:], towers)
    kept = jnp.where(zh == 0, weight_part[:, 0], weight_part[:, 1])
    sent = jnp.where(zh == 0, weight_part[:, 1], weight_part[:, 0]).astype(BF16)
    gain_rows = jnp.pad(two_terms(gain_part), ((0, EXTRA - 2 * towers), (0, 0)))
    sent = jnp.concatenate([sent.reshape(towers * rows, cols), gain_rows], axis=0)
    got = swap(sent, "zh")
    grad_weight = kept + got[: towers * rows].reshape(towers, rows, cols).astype(F32)
    grad_weight = grad_weight.transpose(1, 0, 2)
    grad_gain = joined_terms(gain_rows, towers) + joined_terms(got[towers * rows :], towers)
    return (grad_context, grad_weight, grad_gain)


def solution(mesh):
    finer = Mesh(mesh.devices.reshape(2, 4, 4, 2, 4, 2), DP + SHARD)

    return jax.shard_map(
        local,
        mesh=finer,
        in_specs=(
            P(SHARD, None),
            P(SHARD, DP),
            P(SHARD, DP),
            P(SHARD),
            P(SHARD, None, DP),
            P(None, DP),
        ),
        out_specs=(P(SHARD, DP), P(SHARD, None, DP), P(None, DP)),
        check_vma=False,
    )
```
